32 devices in a mesh: group: 2 (over y), chan: 4 (over z), tm: 2 (over x), beam: 2 (over core).
Axes of the slice: x: 2, y: 2, z: 4, core: 2. Of those that a mesh axis runs over, the one named last changes fastest.
Arguments:
- samples: bfloat16 [1024, 2, 1024, 16], P(('group', 'chan', 'beam'), None, None, 'tm'), parts along dimension 0, may hold values from -6 to 6
- window_taps: float32 [4, 1024], replicated, may hold values from -1 to 1
- sky_model: bfloat16 [1024, 2, 512, 512], P(('group', 'chan', 'tm'), None, 'beam'), parts along dimension 0, may hold values from -0.0234375 to 0.0234375
- prior_gains: float32 [1024, 2, 512], P(('group', 'chan', 'tm')), parts along dimension 0, may hold values from -4.2 to 4.2
- beam_steering: int32 [2, 1024], P(None, ('group', 'beam')), parts along dimension 1, may hold values from 0 to 255
- input_flags: int32 [1024, 512], P(('group', 'chan', 'tm')), parts along dimension 0, may hold values 0 or 1
Outputs:
- visibilities: bfloat16 [1024, 2, 512, 512], P(('group', 'chan', 'tm'), None, 'beam'), parts along dimension 0
- new_gains: float32 [1024, 2, 512], P(('group', 'chan', 'tm'), None, 'beam'), parts along dimension 0
- beam_power: float32 [1024, 512, 16], P(('group', 'chan', 'tm'), 'beam'), parts along dimension 0
The draws below stay inside these ranges and needn't reach their ends.
There are 2 independent parts, one for each index of `group`. The reference program is written for one: setup_inputs(seed, part) draws one part's arguments, and reference() takes and returns one part's arrays. A program takes and returns all parts, laid end to end along the dimension named above; an argument that names none is the same for every part. Nothing has to cross between parts.
All inputs are finite; a program needn't handle non-finite values. No bound on the sum of `input_flags` on one device may be relied on, other than what follows from the above.
Results may differ from the reference program's by a relative error of at most 0.0076.
Values may be sent and summed in bfloat16 or wider, within the bound.
A program may use at most 384 MiB of HBM per device.

```python
import math
import jax
import jax.numpy as jnp
from jax import lax

NIN = 512
NFFT = 1024
NCH = 512
PT = 4
NBEAM = 512
ITERS = 2
FRAMES = 16


def touch_ends(drawn, key, smallest, top_value):
    index_at = [jax.random.randint(jax.random.fold_in(key, axis), (), 0, length) for axis, length in enumerate(drawn.shape)]
    widest = drawn.shape.index(max(drawn.shape))
    next_to = index_at[:widest] + [(index_at[widest] + 1) % drawn.shape[widest]] + index_at[widest + 1:]
    return drawn.at[tuple(index_at)].set(smallest).at[tuple(next_to)].set(top_value)


def shard_levels(own_key, dims, pieces, low, top_value):
    def one(dim, blocks):
        steps = jax.random.uniform(jax.random.fold_in(jax.random.fold_in(own_key, 6), dim), (blocks,), jnp.float32, low / len(pieces), top_value / len(pieces))
        return jnp.repeat(jnp.exp(steps), dims[dim] // blocks).reshape((-1,) + (1,) * (len(dims) - dim - 1))

    level = one(*pieces[0])
    for cut in pieces[1:]:
        level = level * one(*cut)
    return level


def noise(stream_key, dims, spread, bound, cuts=(), kind=jnp.bfloat16):
    array = spread * jax.random.normal(stream_key, dims, jnp.float32)
    if cuts:
        array = array * shard_levels(stream_key, dims, cuts, -0.22, 0.18)
    return jnp.clip(array, -bound, bound).astype(kind)


def setup_inputs(seed: int = 0, part: int = 0) -> dict:
    arg_keys = jax.random.split(jax.random.key(seed), 7)
    part_splits = jax.random.split(jax.random.fold_in(arg_keys[6], part), 7)
    return {
        "samples": noise(part_splits[0], (NIN, 2, NFFT, FRAMES), 1.0, 6.0, ((0, 8), (3, 2))),
        "window_taps": jnp.clip(jax.random.uniform(arg_keys[1], (PT, NFFT), jnp.float32, -1.0, 1.0), -1.0, 1.0),
        "sky_model": noise(part_splits[2], (NCH, 2, NIN, NIN), (NIN * NIN // 4) ** -0.5, 0.0234375, ((0, 8), (2, 2))),
        "prior_gains": noise(part_splits[3], (NCH, 2, NIN), 0.7, 4.2, ((0, 8),), jnp.float32),
        "beam_steering": touch_ends(jax.random.randint(part_splits[4], (2, NBEAM), 0, 256), jax.random.fold_in(part_splits[4], 1), 0, 255).astype(jnp.int32),
        "input_flags": touch_ends((jax.random.randint(part_splits[5], (NCH, NIN), 0, 16) < 15).astype(jnp.int32), jax.random.fold_in(part_splits[5], 1), 0, 1),
    }


damping = 0.5
epsilon = 1e-06

def pfb_table(window_taps, kept_count):
    transform_count = window_taps.shape[1]
    kept = jnp.arange(kept_count, dtype=jnp.int32)
    indices = jnp.arange(transform_count, dtype=jnp.int32)
    phases = (kept[:, None] * indices[None, :] % transform_count).astype(jnp.float32) * (2.0 * math.pi / transform_count)
    cosine = jnp.cos(phases)
    sine_part = jnp.sin(phases)
    real_row = jnp.concatenate([cosine, sine_part], axis=1)
    imag_row = jnp.concatenate([-sine_part, cosine], axis=1)
    base_matrix = jnp.stack([real_row, imag_row], axis=1).reshape(2 * kept_count, 2 * transform_count)
    doubled = jnp.concatenate([window_taps, window_taps], axis=1)
    return (base_matrix[None] * doubled[:, None, :] / math.sqrt(transform_count)).astype(jnp.bfloat16)

def steering_angles(beam_steering, channels, input_count, chan_total):
    positions = jnp.arange(input_count, dtype=jnp.int32)
    column = positions // (input_count // 4)
    within = positions % (input_count // 4)
    phase_index = (beam_steering[0][:, None] * column[None, :] * 64 + beam_steering[1][:, None] * within[None, :]) % 256
    scaled = phase_index[None] * (chan_total + channels)[:, None, None]
    return scaled.astype(jnp.float32) * (2.0 * math.pi / (512 * chan_total))

def reference(samples, window_taps, sky_model, prior_gains, beam_steering, input_flags):
    coeff_table = pfb_table(window_taps, NCH).astype(jnp.float32)
    stacked = samples.reshape(NIN, 2 * NFFT, FRAMES)
    group_size = math.gcd(NIN, 32)
    grouped = stacked.reshape(NIN // group_size, group_size, 2 * NFFT, FRAMES)

    def filter_group(group_block):
        values = jnp.pad(group_block.astype(jnp.float32), ((0, 0), (0, 0), (PT - 1, 0)))
        running = jnp.zeros((group_size, 2 * NCH, FRAMES), jnp.float32)
        for tap_index in range(PT):
            running = running + jnp.einsum('ab,ibf->iaf', coeff_table[tap_index], values[:, :, tap_index:tap_index + FRAMES], precision=lax.Precision.HIGHEST)
        return running.astype(jnp.bfloat16)
    spectra = lax.map(filter_group, grouped).reshape(NIN, NCH, 2, FRAMES)
    by_channel = jnp.transpose(spectra, (1, 0, 2, 3))
    channels = jnp.arange(NCH, dtype=jnp.int32)
    highest = lax.Precision.HIGHEST

    def one_channel(channel_items):
        channel_spectrum, model_part, gains_part, flags_part, channel = channel_items
        values = channel_spectrum.astype(jnp.float32)
        paired = values.reshape(NIN, 2 * FRAMES)
        rotated = jnp.stack([values[:, 1], -values[:, 0]], axis=1).reshape(NIN, 2 * FRAMES)
        vis_real = jnp.dot(paired, paired.T, precision=highest) / FRAMES
        vis_imag = jnp.dot(rotated, paired.T, precision=highest) / FRAMES
        vis_stored = jnp.stack([vis_real, vis_imag]).astype(jnp.bfloat16)
        vis_used = lax.optimization_barrier(vis_stored).astype(jnp.float32)
        model_values = model_part.astype(jnp.float32)
        weighted_real = vis_used[0] * model_values[0] + vis_used[1] * model_values[1]
        weighted_imag = vis_used[1] * model_values[0] - vis_used[0] * model_values[1]
        model_power = model_values[0] * model_values[0] + model_values[1] * model_values[1]
        weights = flags_part.astype(jnp.float32)
        current = gains_part
        for step_index in range(ITERS):
            masked_real = current[0] * weights
            masked_imag = current[1] * weights
            numer_real = jnp.dot(weighted_real, masked_real, precision=highest) - jnp.dot(weighted_imag, masked_imag, precision=highest)
            numer_imag = jnp.dot(weighted_real, masked_imag, precision=highest) + jnp.dot(weighted_imag, masked_real, precision=highest)
            denom = jnp.dot(model_power, weights * (current[0] * current[0] + current[1] * current[1]), precision=highest) + epsilon
            current = damping * current + (1.0 - damping) * jnp.stack([numer_real / denom, numer_imag / denom])
        angles = steering_angles(beam_steering, channel[None], NIN, NCH)[0]
        cosine = jnp.cos(angles)
        sine_part = jnp.sin(angles)
        scale_factor = 1.0 / math.sqrt(NIN)
        gain_real = (gains_part[0] * weights)[None, :]
        gain_imaginary = (gains_part[1] * weights)[None, :]
        steering_real = ((gain_real * cosine - gain_imaginary * sine_part) * scale_factor).astype(jnp.bfloat16).astype(jnp.float32)
        steering_imaginary = ((gain_real * sine_part + gain_imaginary * cosine) * scale_factor).astype(jnp.bfloat16).astype(jnp.float32)
        volt_real = jnp.dot(steering_real, values[:, 0], precision=highest) - jnp.dot(steering_imaginary, values[:, 1], precision=highest)
        volt_imag = jnp.dot(steering_real, values[:, 1], precision=highest) + jnp.dot(steering_imaginary, values[:, 0], precision=highest)
        power = volt_real * volt_real + volt_imag * volt_imag
        return (vis_stored, current, power)
    results = lax.map(one_channel, (by_channel, sky_model, prior_gains, input_flags, channels))
    return (results[0], results[1], results[2])
```

```python
import functools
import math

import jax
import jax.numpy as jnp
from jax import lax
from jax.experimental import pallas as pl
from jax.experimental.pallas import tpu as pltpu
from jax.sharding import PartitionSpec as P

NCH = 512
ITERS = 2

damping = 0.5
epsilon = 1e-06
F32 = jnp.float32
BF16 = jnp.bfloat16


def from_behind(block, axis, distance):
    devices = range(lax.axis_size(axis))
    route = [(i - distance, i) for i in devices if i - distance in devices]
    return lax.ppermute(block, axis, route)


def unit_rows(rows, columns, transform_count):
    phases = (rows[:, None] * columns[None, :] % transform_count).astype(F32) * (
        2.0 * math.pi / transform_count
    )
    return jnp.cos(phases), jnp.sin(phases)


def transform_table(kept_count, transform_count):
    fine = 1 << ((kept_count.bit_length() - 1) // 2)
    coarse = kept_count // fine
    columns = jnp.arange(transform_count, dtype=jnp.int32)
    high_c, high_s = unit_rows(jnp.arange(coarse, dtype=jnp.int32) * fine, columns, transform_count)
    low_c, low_s = unit_rows(jnp.arange(fine, dtype=jnp.int32), columns, transform_count)
    high_c, high_s, low_c, low_s = lax.optimization_barrier((high_c, high_s, low_c, low_s))
    scale = 1.0 / math.sqrt(transform_count)
    high_c, high_s = high_c * scale, high_s * scale
    cosine = high_c[:, None] * low_c[None] - high_s[:, None] * low_s[None]
    sine = high_s[:, None] * low_c[None] + high_c[:, None] * low_s[None]
    cosine = cosine.reshape(kept_count, transform_count).astype(BF16)
    sine = sine.reshape(kept_count, transform_count).astype(BF16)
    real_row = jnp.concatenate([cosine, sine], axis=1)
    imag_row = jnp.concatenate([-sine, cosine], axis=1)
    return real_row, imag_row


def filter_bank(samples, window_taps, kept_count):
    local_inputs, _, transform_count, frames = samples.shape
    tap_count = window_taps.shape[0]
    framed = jnp.transpose(samples, (3, 0, 1, 2))
    previous = from_behind(framed[frames - tap_count + 1 :], "tm", 1)
    extended = jnp.concatenate([previous, framed], axis=0).astype(F32)
    windowed = sum(
        extended[tap : tap + frames] * window_taps[tap][None, None, None, :]
        for tap in range(tap_count)
    )
    windowed = windowed.astype(BF16).reshape(frames * local_inputs, 2 * transform_count)
    tables = transform_table(kept_count, transform_count)
    parts = [
        lax.dot_general(t, windowed, (((1,), (1,)), ((), ())), preferred_element_type=F32)
        for t in tables
    ]
    return jnp.stack([p.astype(BF16) for p in parts], axis=1)


NT = (((1,), (1,)), ((), ()))
TN = (((0,), (0,)), ((), ()))


def dot_nt(a, b):
    return lax.dot_general(a, b, NT, preferred_element_type=F32)


def gain_update(x, own, model, gains, older, flags):
    half = x.shape[0] // 2
    frames = half
    hr, hi = gains[0:1] * flags, gains[1:2] * flags
    xr, xi = x[:half].astype(F32), x[half:].astype(F32)
    y = jnp.concatenate([xr * hr + xi * hi, xi * hr - xr * hi], axis=0).astype(BF16)
    a = dot_nt(y, model[0])
    b = dot_nt(y, model[1])
    zr = a[:half] - b[half:]
    zi = a[half:] + b[:half]
    pr, pi = own[:half].astype(F32), own[half:].astype(F32)
    numer_r = jnp.sum(pr * zr + pi * zi, axis=0, keepdims=True) * (1.0 / frames)
    numer_i = jnp.sum(pi * zr - pr * zi, axis=0, keepdims=True) * (1.0 / frames)
    power = flags * (gains[0:1] * gains[0:1] + gains[1:2] * gains[1:2])
    top = power.astype(BF16)
    rest = (power - top.astype(F32)).astype(BF16)
    mr, mi = model[0].astype(F32), model[1].astype(F32)
    model_power = (mr * mr + mi * mi).astype(BF16)
    both = jnp.concatenate(
        [jnp.broadcast_to(top.astype(F32), (8, top.shape[1])),
         jnp.broadcast_to(rest.astype(F32), (8, top.shape[1]))], axis=0
    ).astype(BF16)
    d = dot_nt(both, model_power)
    denom = d[0:1] + d[8:9] + epsilon
    update = jnp.concatenate([numer_r, numer_i], axis=0) / denom
    return damping * older + (1.0 - damping) * update


def correlate_kernel(beam_ref, x_ref, own_ref, model_ref, gain_ref, older_ref, flag_ref, vis_ref, new_ref):
    for c in range(x_ref.shape[0]):
        x, own = x_ref[c], own_ref[c]
        half = x.shape[0] // 2
        scale = 1.0 / half
        vis_ref[c, 0] = (
            lax.dot_general(own, x, TN, preferred_element_type=F32) * scale
        ).astype(BF16)
        rotated = jnp.concatenate([own[half:], -own[:half]], axis=0)
        vis_ref[c, 1] = (
            lax.dot_general(rotated, x, TN, preferred_element_type=F32) * scale
        ).astype(BF16)
        new_ref[c] = gain_update(
            x, own, model_ref.at[c], gain_ref[c], older_ref[c], flag_ref[c].astype(F32)
        )


def update_kernel(beam_ref, x_ref, own_ref, model_ref, gain_ref, older_ref, flag_ref, new_ref):
    for c in range(x_ref.shape[0]):
        new_ref[c] = gain_update(
            x_ref[c], own_ref[c], model_ref.at[c], gain_ref[c], older_ref[c],
            flag_ref[c].astype(F32),
        )


def gain_call(correlate, beam_index, x, model, gains, older, flags):
    channels, rows, inputs = x.shape
    mine = model.shape[2]
    block = math.gcd(channels, 4)
    whole = lambda *shape: pl.BlockSpec((block, *shape), lambda c, b: (c,) + (0,) * len(shape))
    part = lambda r: pl.BlockSpec((block, r, mine), lambda c, b: (c, 0, b[0]))
    older_spec = part(2) if older.shape[2] == inputs else whole(2, mine)
    new_shape = jax.ShapeDtypeStruct((channels, 2, mine), F32)
    if correlate:
        out_shape = [jax.ShapeDtypeStruct(model.shape, BF16), new_shape]
        out_specs = [whole(2, mine, inputs), whole(2, mine)]
    else:
        out_shape, out_specs = new_shape, whole(2, mine)
    return pl.pallas_call(
        correlate_kernel if correlate else update_kernel,
        out_shape=out_shape,
        grid_spec=pltpu.PrefetchScalarGridSpec(
            num_scalar_prefetch=1,
            grid=(channels // block,),
            in_specs=[whole(rows, inputs), part(rows), whole(2, mine, inputs), whole(2, inputs),
                      older_spec, whole(1, inputs)],
            out_specs=out_specs,
        ),
        cost_estimate=pl.CostEstimate(
            flops=8 * channels * mine * inputs * rows,
            bytes_accessed=(4 + 4 * correlate) * model.size // 2,
            transcendentals=0,
        ),
        name="correlate" if correlate else "update",
    )(beam_index, x, x, model, gains, older, flags)


def beam_kernel(base_ref, x_ref, gain_ref, flag_ref, bits_ref, power_ref, cur_r, cur_i, one_r, one_i, rot_r, rot_i, *, unit, scale):
    block = x_ref.shape[0]
    beams, inputs = cur_r.shape
    step = 16

    @pl.when(pl.program_id(0) == 0)
    def _():
        first = base_ref[0]

        def fill(r, carry):
            rows = pl.ds(r * 8, 8)
            bits = bits_ref[rows, :]
            angle = (bits * first).astype(F32) * unit
            cur_r[rows, :] = jnp.cos(angle)
            cur_i[rows, :] = jnp.sin(angle)
            small = bits.astype(F32) * unit
            one_r[rows, :] = jnp.cos(small)
            one_i[rows, :] = jnp.sin(small)
            return carry

        lax.fori_loop(0, beams // 8, fill, 0)

    def turn(r, carry):
        rows = pl.ds(r * step, step)
        ar, ai = cur_r[rows, :], cur_i[rows, :]
        br, bi = one_r[rows, :], one_i[rows, :]
        for c in range(block):
            rot_r[c, rows, :] = ar.astype(BF16)
            rot_i[c, rows, :] = ai.astype(BF16)
            ar, ai = ar * br - ai * bi, ar * bi + ai * br
        cur_r[rows, :] = ar
        cur_i[rows, :] = ai
        return carry

    lax.fori_loop(0, beams // step, turn, 0)
    for c in range(block):
        x, gains = x_ref[c], gain_ref[c]
        flags = flag_ref[c].astype(F32) * scale
        half = x.shape[0] // 2
        hr, hi = gains[0:1] * flags, gains[1:2] * flags
        xr, xi = x[:half].astype(F32), x[half:].astype(F32)
        y = jnp.concatenate([xr * hr - xi * hi, xi * hr + xr * hi], axis=0)
        top = y.astype(BF16)
        rest = (y - top.astype(F32)).astype(BF16)
        both = jnp.concatenate([top, rest], axis=0)
        a = dot_nt(both, rot_r[c])
        b = dot_nt(both, rot_i[c])
        a = a[: 2 * half] + a[2 * half :]
        b = b[: 2 * half] + b[2 * half :]
        vr = a[:half] - b[half:]
        vi = a[half:] + b[:half]
        power_ref[c] = vr * vr + vi * vi


def form_beams(x, gains, flags, beam_steering, first_channel, chan_total):
    channels, rows, inputs = x.shape
    beams = beam_steering.shape[1]
    positions = jnp.arange(inputs, dtype=jnp.int32)
    column = positions // (inputs // 4)
    within = positions % (inputs // 4)
    bits = (
        beam_steering[0][:, None] * column[None, :] * 64
        + beam_steering[1][:, None] * within[None, :]
    ) % 256
    block = math.gcd(channels, 8)
    whole = lambda *shape: pl.BlockSpec((block, *shape), lambda c, b: (c,) + (0,) * len(shape))
    kernel = functools.partial(
        beam_kernel, unit=2.0 * math.pi / (512 * chan_total), scale=1.0 / math.sqrt(inputs)
    )
    return pl.pallas_call(
        kernel,
        out_shape=jax.ShapeDtypeStruct((channels, rows // 2, beams), F32),
        grid_spec=pltpu.PrefetchScalarGridSpec(
            num_scalar_prefetch=1,
            grid=(channels // block,),
            in_specs=[whole(rows, inputs), whole(2, inputs), whole(1, inputs),
                      pl.BlockSpec((beams, inputs), lambda c, b: (0, 0))],
            out_specs=whole(rows // 2, beams),
            scratch_shapes=[pltpu.VMEM((beams, inputs), F32)] * 4
            + [pltpu.VMEM((block, beams, inputs), BF16)] * 2,
        ),
        cost_estimate=pl.CostEstimate(
            flops=8 * channels * beams * inputs * rows,
            bytes_accessed=2 * x.size * 20,
            transcendentals=0,
        ),
        name="beams",
    )(jnp.reshape(chan_total + first_channel, (1,)), x, gains, flags, bits)


def shards(samples, window_taps, sky_model, prior_gains, beam_steering, input_flags):
    local_inputs = samples.shape[0]
    frames = samples.shape[3]
    kept_count = NCH
    time_count = lax.axis_size("tm")
    chan_count = lax.axis_size("chan")
    beam_count = lax.axis_size("beam")
    owners = time_count * chan_count
    chan_local = kept_count // owners
    spectra = filter_bank(samples, window_taps, kept_count)
    spectra = spectra.reshape(owners, chan_local, 2, frames * local_inputs)
    mixed = lax.all_to_all(spectra, ("chan", "tm"), split_axis=0, concat_axis=0, tiled=True)
    joined = lax.all_gather(mixed, "beam", axis=0)
    joined = joined.reshape(
        beam_count, chan_count, time_count, chan_local, 2, frames, local_inputs
    )
    x = jnp.transpose(joined, (3, 4, 2, 5, 1, 0, 6)).reshape(
        chan_local, 2 * time_count * frames, chan_count * beam_count * local_inputs
    )
    flags = input_flags[:, None, :]
    beam_index = jnp.reshape(lax.axis_index("beam"), (1,)).astype(jnp.int32)
    visibilities, updated = gain_call(
        True, beam_index, x, sky_model, prior_gains, prior_gains, flags
    )
    first_channel = (lax.axis_index("chan") * time_count + lax.axis_index("tm")) * chan_local
    beam_power = form_beams(
        x, prior_gains, flags, beam_steering, first_channel.astype(jnp.int32), kept_count
    )
    for _ in range(ITERS - 1):
        current = lax.all_gather(updated, "beam", axis=2, tiled=True)
        updated = gain_call(False, beam_index, x, sky_model, current, updated, flags)
    return (visibilities, updated, jnp.transpose(beam_power, (0, 2, 1)))


def solution(mesh):
    return jax.shard_map(
        shards,
        mesh=mesh,
        in_specs=(
            P(("group", "chan", "beam"), None, None, "tm"),
            P(),
            P(("group", "chan", "tm"), None, "beam", None),
            P(("group", "chan", "tm"), None, None),
            P(None, ("group", "beam")),
            P(("group", "chan", "tm"), None),
        ),
        out_specs=(
            P(("group", "chan", "tm"), None, "beam", None),
            P(("group", "chan", "tm"), None, "beam"),
            P(("group", "chan", "tm"), "beam", None),
        ),
        check_vma=False,
    )
```

```python
import functools
import math

import jax
import jax.numpy as jnp
from jax import lax
from jax.experimental import pallas as pl
from jax.experimental.pallas import tpu as pltpu
from jax.sharding import PartitionSpec as P

NCH = 512
ITERS = 2

damping = 0.5
epsilon = 1e-06
F32 = jnp.float32
BF16 = jnp.bfloat16


def from_behind(block, axis, distance):
    devices = range(lax.axis_size(axis))
    route = [(i - distance, i) for i in devices if i - distance in devices]
    return lax.ppermute(block, axis, route)


def unit_rows(rows, columns, transform_count):
    phases = (rows[:, None] * columns[None, :] % transform_count).astype(F32) * (
        2.0 * math.pi / transform_count
    )
    return jnp.cos(phases), jnp.sin(phases)


def transform_table(kept_count, transform_count):
    fine = 1 << ((kept_count.bit_length() - 1) // 2)
    coarse = kept_count // fine
    columns = jnp.arange(transform_count, dtype=jnp.int32)
    high_c, high_s = unit_rows(jnp.arange(coarse, dtype=jnp.int32) * fine, columns, transform_count)
    low_c, low_s = unit_rows(jnp.arange(fine, dtype=jnp.int32), columns, transform_count)
    high_c, high_s, low_c, low_s = lax.optimization_barrier((high_c, high_s, low_c, low_s))
    scale = 1.0 / math.sqrt(transform_count)
    high_c, high_s = high_c * scale, high_s * scale
    cosine = high_c[:, None] * low_c[None] - high_s[:, None] * low_s[None]
    sine = high_s[:, None] * low_c[None] + high_c[:, None] * low_s[None]
    cosine = cosine.reshape(kept_count, transform_count).astype(BF16)
    sine = sine.reshape(kept_count, transform_count).astype(BF16)
    return cosine, sine


def filter_bank(samples, window_taps, kept_count, beside):
    local_inputs, _, transform_count, frames = samples.shape
    tap_count = window_taps.shape[0]
    framed = jnp.transpose(samples, (3, 1, 0, 2))
    previous = from_behind(framed[frames - tap_count + 1 :], "tm", 1)
    previous, beside = lax.optimization_barrier((previous, beside))
    extended = jnp.concatenate([previous, framed], axis=0).astype(F32)
    windowed = sum(
        extended[tap : tap + frames] * window_taps[tap][None, None, None, :]
        for tap in range(tap_count)
    )
    windowed = windowed.astype(BF16)
    real_in = windowed[:, 0].reshape(frames * local_inputs, transform_count)
    imag_in = windowed[:, 1].reshape(frames * local_inputs, transform_count)
    cosine, sine = transform_table(kept_count, transform_count)
    real = dot_nt(cosine, real_in) + dot_nt(sine, imag_in)
    imag = dot_nt(cosine, imag_in) - dot_nt(sine, real_in)
    return real.astype(BF16), imag.astype(BF16), beside


NT = (((1,), (1,)), ((), ()))
TN = (((0,), (0,)), ((), ()))


def dot_nt(a, b):
    return lax.dot_general(a, b, NT, preferred_element_type=F32)


def numerators(x, own, model, gains, flags):
    half = x.shape[0] // 2
    hr, hi = gains[0:1] * flags, gains[1:2] * flags
    xr, xi = x[:half].astype(F32), x[half:].astype(F32)
    y = jnp.concatenate([xr * hr + xi * hi, xi * hr - xr * hi], axis=0).astype(BF16)
    a = dot_nt(y, model[0])
    b = dot_nt(y, model[1])
    zr = a[:half] - b[half:]
    zi = a[half:] + b[:half]
    pr, pi = own[:half].astype(F32), own[half:].astype(F32)
    numer_r = jnp.sum(pr * zr + pi * zi, axis=0, keepdims=True) * (1.0 / half)
    numer_i = jnp.sum(pi * zr - pr * zi, axis=0, keepdims=True) * (1.0 / half)
    return jnp.concatenate([numer_r, numer_i], axis=0)


def denominators(model, gains, flags):
    power = flags * (gains[0:1] * gains[0:1] + gains[1:2] * gains[1:2])
    top = power.astype(BF16).astype(F32)
    wide = (8, top.shape[1])
    both = jnp.concatenate(
        [jnp.broadcast_to(top, wide), jnp.broadcast_to(power - top, wide)], axis=0
    ).astype(BF16)
    mr, mi = model[0].astype(F32), model[1].astype(F32)
    d = dot_nt(both, (mr * mr + mi * mi).astype(BF16))
    return d[0:1] + d[8:9] + epsilon


def damped(older, numer, denom):
    return damping * older + (1.0 - damping) * (numer / denom)


def denominator_kernel(model_ref, gain_ref, flag_ref, out_ref):
    for c in range(model_ref.shape[0]):
        out_ref[c] = denominators(model_ref.at[c], gain_ref[c], flag_ref[c].astype(F32))


def first_denominators(model, gains, flags):
    channels, _, mine, inputs = model.shape
    block = math.gcd(channels, 4)
    whole = lambda *shape: pl.BlockSpec((block, *shape), lambda c: (c,) + (0,) * len(shape))
    return pl.pallas_call(
        denominator_kernel,
        out_shape=jax.ShapeDtypeStruct((channels, 1, mine), F32),
        grid=(channels // block,),
        in_specs=[whole(2, mine, inputs), whole(2, inputs), whole(1, inputs)],
        out_specs=whole(1, mine),
        cost_estimate=pl.CostEstimate(
            flops=16 * model.size, bytes_accessed=2 * model.size, transcendentals=0
        ),
        name="denominators",
    )(model, gains, flags)


def correlate_kernel(beam_ref, x_ref, own_ref, model_ref, gain_ref, older_ref, flag_ref, denom_ref, vis_ref, new_ref):
    for c in range(x_ref.shape[0]):
        x, own = x_ref[c], own_ref[c]
        half = x.shape[0] // 2
        scale = 1.0 / half
        vis_ref[c, 0] = (
            lax.dot_general(own, x, TN, preferred_element_type=F32) * scale
        ).astype(BF16)
        rotated = jnp.concatenate([own[half:], -own[:half]], axis=0)
        vis_ref[c, 1] = (
            lax.dot_general(rotated, x, TN, preferred_element_type=F32) * scale
        ).astype(BF16)
        numer = numerators(x, own, model_ref.at[c], gain_ref[c], flag_ref[c].astype(F32))
        new_ref[c] = damped(older_ref[c], numer, denom_ref[c])


def update_kernel(beam_ref, x_ref, own_ref, model_ref, gain_ref, older_ref, flag_ref, new_ref):
    for c in range(x_ref.shape[0]):
        model, gains, flags = model_ref.at[c], gain_ref[c], flag_ref[c].astype(F32)
        numer = numerators(x_ref[c], own_ref[c], model, gains, flags)
        new_ref[c] = damped(older_ref[c], numer, denominators(model, gains, flags))


def turn_kernel(in_ref, out_ref, rows_ref, *, inputs):
    beams, chans, times, paired, lanes = in_ref.shape
    frames = lanes // inputs
    planes = times * frames
    width = rows_ref.shape[2]
    for b in range(beams):
        for z in range(chans):
            column = (z * beams + b) * inputs
            at = column % width
            for t in range(times):
                slab = in_ref[b, z, t].astype(F32)
                for f in range(frames):
                    plane = t * frames + f
                    rows_ref[
                        column // width, plane * paired : (plane + 1) * paired, at : at + inputs
                    ] = slab[:, f * inputs : (f + 1) * inputs]

    def gather(k, carry):
        for q in range(rows_ref.shape[0]):
            parts = [
                rows_ref.at[q][pl.ds(s * (paired // 2) + k, planes, stride=paired), :]
                for s in range(2)
            ]
            out_ref[k, :, q * width : (q + 1) * width] = jnp.concatenate(parts, axis=0).astype(BF16)
        return carry

    lax.fori_loop(0, paired // 2, gather, 0)


def turn(joined, inputs):
    beams, chans, times, paired, lanes = joined.shape
    planes = times * (lanes // inputs)
    total = chans * beams * inputs
    width = 128
    return pl.pallas_call(
        functools.partial(turn_kernel, inputs=inputs),
        out_shape=jax.ShapeDtypeStruct((paired // 2, 2 * planes, total), BF16),
        scratch_shapes=[pltpu.VMEM((total // width, planes * paired, width), F32)],
        cost_estimate=pl.CostEstimate(
            flops=0, bytes_accessed=8 * joined.size, transcendentals=0
        ),
        name="turn",
    )(joined)


def gain_call(beam_index, x, model, gains, older, flags, denom=None):
    correlate = denom is not None
    channels, rows, inputs = x.shape
    mine = model.shape[2]
    block = math.gcd(channels, 4)
    whole = lambda *shape: pl.BlockSpec((block, *shape), lambda c, b: (c,) + (0,) * len(shape))
    part = lambda r: pl.BlockSpec((block, r, mine), lambda c, b: (c, 0, b[0]))
    older_spec = part(2) if older.shape[2] == inputs else whole(2, mine)
    new_shape = jax.ShapeDtypeStruct((channels, 2, mine), F32)
    if correlate:
        out_shape = [jax.ShapeDtypeStruct(model.shape, BF16), new_shape]
        out_specs = [whole(2, mine, inputs), whole(2, mine)]
    else:
        out_shape, out_specs = new_shape, whole(2, mine)
    return pl.pallas_call(
        correlate_kernel if correlate else update_kernel,
        out_shape=out_shape,
        grid_spec=pltpu.PrefetchScalarGridSpec(
            num_scalar_prefetch=1,
            grid=(channels // block,),
            in_specs=[whole(rows, inputs), part(rows), whole(2, mine, inputs), whole(2, inputs),
                      older_spec, whole(1, inputs)] + [whole(1, mine)] * correlate,
            out_specs=out_specs,
        ),
        cost_estimate=pl.CostEstimate(
            flops=8 * channels * mine * inputs * rows,
            bytes_accessed=(4 + 4 * correlate) * model.size // 2,
            transcendentals=0,
        ),
        name="correlate" if correlate else "update",
    )(beam_index, x, x, model, gains, older, flags, *([denom] if correlate else []))


def steering_kernel(base_ref, bits_ref, rot_r, rot_i, cur_r, cur_i, one_r, one_i, *, unit):
    block = rot_r.shape[0]
    beams, inputs = cur_r.shape
    step = 16

    @pl.when(pl.program_id(0) == 0)
    def _():
        first = base_ref[0]

        def fill(r, carry):
            rows = pl.ds(r * 8, 8)
            bits = bits_ref[rows, :]
            angle = (bits * first).astype(F32) * unit
            cur_r[rows, :] = jnp.cos(angle)
            cur_i[rows, :] = jnp.sin(angle)
            small = bits.astype(F32) * unit
            one_r[rows, :] = jnp.cos(small)
            one_i[rows, :] = jnp.sin(small)
            return carry

        lax.fori_loop(0, beams // 8, fill, 0)

    def advance(r, carry):
        rows = pl.ds(r * step, step)
        ar, ai = cur_r[rows, :], cur_i[rows, :]
        br, bi = one_r[rows, :], one_i[rows, :]
        for c in range(block):
            rot_r[c, rows, :] = ar.astype(BF16)
            rot_i[c, rows, :] = ai.astype(BF16)
            ar, ai = ar * br - ai * bi, ar * bi + ai * br
        cur_r[rows, :] = ar
        cur_i[rows, :] = ai
        return carry

    lax.fori_loop(0, beams // step, advance, 0)


def steering(beam_steering, inputs, channels, first_channel, chan_total):
    beams = beam_steering.shape[1]
    positions = jnp.arange(inputs, dtype=jnp.int32)
    column = positions // (inputs // 4)
    within = positions % (inputs // 4)
    bits = (
        beam_steering[0][:, None] * column[None, :] * 64
        + beam_steering[1][:, None] * within[None, :]
    ) % 256
    block = math.gcd(channels, 8)
    rot = jax.ShapeDtypeStruct((channels, beams, inputs), BF16)
    rot_spec = pl.BlockSpec((block, beams, inputs), lambda c, b: (c, 0, 0))
    return pl.pallas_call(
        functools.partial(steering_kernel, unit=2.0 * math.pi / (512 * chan_total)),
        out_shape=[rot, rot],
        grid_spec=pltpu.PrefetchScalarGridSpec(
            num_scalar_prefetch=1,
            grid=(channels // block,),
            in_specs=[pl.BlockSpec((beams, inputs), lambda c, b: (0, 0))],
            out_specs=[rot_spec, rot_spec],
            scratch_shapes=[pltpu.VMEM((beams, inputs), F32)] * 4,
        ),
        cost_estimate=pl.CostEstimate(
            flops=8 * rot.size, bytes_accessed=6 * rot.size, transcendentals=0
        ),
        name="steering",
    )(jnp.reshape(chan_total + first_channel, (1,)), bits)


def beam_kernel(x_ref, gain_ref, flag_ref, rot_r, rot_i, power_ref, *, scale):
    for c in range(x_ref.shape[0]):
        x, gains = x_ref[c], gain_ref[c]
        flags = flag_ref[c].astype(F32) * scale
        half = x.shape[0] // 2
        hr, hi = gains[0:1] * flags, gains[1:2] * flags
        xr, xi = x[:half].astype(F32), x[half:].astype(F32)
        y = jnp.concatenate([xr * hr - xi * hi, xi * hr + xr * hi], axis=0)
        top = y.astype(BF16)
        rest = (y - top.astype(F32)).astype(BF16)
        both = jnp.concatenate([top, rest], axis=0)
        a = dot_nt(both, rot_r[c])
        b = dot_nt(both, rot_i[c])
        a = a[: 2 * half] + a[2 * half :]
        b = b[: 2 * half] + b[2 * half :]
        vr = a[:half] - b[half:]
        vi = a[half:] + b[:half]
        power_ref[c] = vr * vr + vi * vi


def form_beams(x, gains, flags, rot_r, rot_i):
    channels, rows, inputs = x.shape
    beams = rot_r.shape[1]
    block = math.gcd(channels, 4)
    whole = lambda *shape: pl.BlockSpec((block, *shape), lambda c: (c,) + (0,) * len(shape))
    return pl.pallas_call(
        functools.partial(beam_kernel, scale=1.0 / math.sqrt(inputs)),
        out_shape=jax.ShapeDtypeStruct((channels, rows // 2, beams), F32),
        grid=(channels // block,),
        in_specs=[whole(rows, inputs), whole(2, inputs), whole(1, inputs),
                  whole(beams, inputs), whole(beams, inputs)],
        out_specs=whole(rows // 2, beams),
        cost_estimate=pl.CostEstimate(
            flops=8 * channels * beams * inputs * rows,
            bytes_accessed=4 * rot_r.size, transcendentals=0,
        ),
        name="beams",
    )(x, gains, flags, rot_r, rot_i)


def shards(samples, window_taps, sky_model, prior_gains, beam_steering, input_flags):
    local_inputs = samples.shape[0]
    frames = samples.shape[3]
    kept_count = NCH
    time_count = lax.axis_size("tm")
    chan_count = lax.axis_size("chan")
    beam_count = lax.axis_size("beam")
    owners = time_count * chan_count
    chan_local = kept_count // owners
    first_channel = (lax.axis_index("chan") * time_count + lax.axis_index("tm")) * chan_local
    input_count = local_inputs * chan_count * beam_count
    rot_r, rot_i = steering(
        beam_steering, input_count, chan_local, first_channel.astype(jnp.int32), kept_count
    )
    flags = input_flags[:, None, :]
    denom = first_denominators(sky_model, prior_gains, flags)
    real, imag, (rot_r, rot_i) = filter_bank(samples, window_taps, kept_count, (rot_r, rot_i))
    by_owner = (owners, chan_local, frames * local_inputs)
    spectra = jnp.concatenate([real.reshape(by_owner), imag.reshape(by_owner)], axis=1)
    mixed = lax.all_to_all(spectra, ("chan", "tm"), split_axis=0, concat_axis=0, tiled=True)
    joined = lax.all_gather(mixed, "beam", axis=0)
    joined = joined.reshape(beam_count, chan_count, time_count, *joined.shape[2:])
    x = turn(joined, local_inputs)
    beam_index = jnp.reshape(lax.axis_index("beam"), (1,)).astype(jnp.int32)
    visibilities, updated = gain_call(
        beam_index, x, sky_model, prior_gains, prior_gains, flags, denom
    )
    beam_power = form_beams(x, prior_gains, flags, rot_r, rot_i)
    for _ in range(ITERS - 1):
        current = lax.all_gather(updated, "beam", axis=2, tiled=True)
        updated = gain_call(beam_index, x, sky_model, current, updated, flags)
    return (visibilities, updated, jnp.transpose(beam_power, (0, 2, 1)))


def solution(mesh):
    return jax.shard_map(
        shards,
        mesh=mesh,
        in_specs=(
            P(("group", "chan", "beam"), None, None, "tm"),
            P(),
            P(("group", "chan", "tm"), None, "beam", None),
            P(("group", "chan", "tm"), None, None),
            P(None, ("group", "beam")),
            P(("group", "chan", "tm"), None),
        ),
        out_specs=(
            P(("group", "chan", "tm"), None, "beam", None),
            P(("group", "chan", "tm"), None, "beam"),
            P(("group", "chan", "tm"), "beam", None),
        ),
        check_vma=False,
    )
```

```python
import functools
import math

import jax
import jax.numpy as jnp
from jax import lax
from jax.experimental import pallas as pl
from jax.experimental.pallas import tpu as pltpu
from jax.sharding import PartitionSpec as P

NCH = 512
ITERS = 2


damping = 0.5
epsilon = 1e-06
F32 = jnp.float32
BF16 = jnp.bfloat16


def from_behind(block, axis, distance):
    devices = range(lax.axis_size(axis))
    route = [(i - distance, i) for i in devices if i - distance in devices]
    return lax.ppermute(block, axis, route)


def unit_rows(rows, columns, transform_count):
    phases = (rows[:, None] * columns[None, :] % transform_count).astype(F32) * (
        2.0 * math.pi / transform_count
    )
    return jnp.cos(phases), jnp.sin(phases)


def transform_table(kept_count, transform_count):
    fine = 1 << ((kept_count.bit_length() - 1) // 2)
    coarse = kept_count // fine
    columns = jnp.arange(transform_count, dtype=jnp.int32)
    high_c, high_s = unit_rows(jnp.arange(coarse, dtype=jnp.int32) * fine, columns, transform_count)
    low_c, low_s = unit_rows(jnp.arange(fine, dtype=jnp.int32), columns, transform_count)
    high_c, high_s, low_c, low_s = lax.optimization_barrier((high_c, high_s, low_c, low_s))
    scale = 1.0 / math.sqrt(transform_count)
    high_c, high_s = high_c * scale, high_s * scale
    cosine = high_c[:, None] * low_c[None] - high_s[:, None] * low_s[None]
    sine = high_s[:, None] * low_c[None] + high_c[:, None] * low_s[None]
    cosine = cosine.reshape(kept_count, transform_count).astype(BF16)
    sine = sine.reshape(kept_count, transform_count).astype(BF16)
    return cosine, sine


def filter_bank(samples, window_taps, kept_count, beside):
    local_inputs, _, transform_count, frames = samples.shape
    tap_count = window_taps.shape[0]
    framed = jnp.transpose(samples, (3, 1, 0, 2))
    previous = from_behind(framed[frames - tap_count + 1 :], "tm", 1)
    previous, beside = lax.optimization_barrier((previous, beside))
    extended = jnp.concatenate([previous, framed], axis=0).astype(F32)
    windowed = sum(
        extended[tap : tap + frames] * window_taps[tap][None, None, None, :]
        for tap in range(tap_count)
    )
    windowed = windowed.astype(BF16)
    real_in = windowed[:, 0].reshape(frames * local_inputs, transform_count)
    imag_in = windowed[:, 1].reshape(frames * local_inputs, transform_count)
    cosine, sine = transform_table(kept_count, transform_count)
    real = dot_nt(cosine, real_in) + dot_nt(sine, imag_in)
    imag = dot_nt(cosine, imag_in) - dot_nt(sine, real_in)
    return real.astype(BF16), imag.astype(BF16), beside


NT = (((1,), (1,)), ((), ()))
TN = (((0,), (0,)), ((), ()))


def dot_nt(a, b):
    return lax.dot_general(a, b, NT, preferred_element_type=F32)


def complex_product(left_r, left_i, vr, vi):
    straight = jnp.concatenate([vr, vi], axis=0).astype(BF16)
    crossed = jnp.concatenate([-vi, vr], axis=0).astype(BF16)
    return (dot_nt(left_r, straight) + dot_nt(left_i, crossed)).T


def numerators(x, own, model, gains, flags):
    half = x.shape[0] // 2
    hr, hi = gains[0:1] * flags, gains[1:2] * flags
    xr, xi = x[:half].astype(F32), x[half:].astype(F32)
    z = complex_product(model[0], model[1], xr * hr + xi * hi, xi * hr - xr * hi)
    zr, zi = z[:half], z[half:]
    pr, pi = own[:half].astype(F32), own[half:].astype(F32)
    numer_r = jnp.sum(pr * zr + pi * zi, axis=0, keepdims=True) * (1.0 / half)
    numer_i = jnp.sum(pi * zr - pr * zi, axis=0, keepdims=True) * (1.0 / half)
    return jnp.concatenate([numer_r, numer_i], axis=0)


def denominators(model, gains, flags):
    power = flags * (gains[0:1] * gains[0:1] + gains[1:2] * gains[1:2])
    top = power.astype(BF16).astype(F32)
    wide = (8, top.shape[1])
    both = jnp.concatenate(
        [jnp.broadcast_to(top, wide), jnp.broadcast_to(power - top, wide)], axis=0
    ).astype(BF16)
    mr, mi = model[0], model[1]
    d = dot_nt(mr * mr + mi * mi, both).T
    return d[0:1] + d[8:9] + epsilon


def damped(older, numer, denom):
    return damping * older + (1.0 - damping) * (numer / denom)


def denominator_kernel(model_ref, gain_ref, flag_ref, out_ref):
    for c in range(model_ref.shape[0]):
        out_ref[c] = denominators(model_ref.at[c], gain_ref[c], flag_ref[c].astype(F32))


def first_denominators(model, gains, flags):
    channels, _, mine, inputs = model.shape
    block = math.gcd(channels, 4)
    whole = lambda *shape: pl.BlockSpec((block, *shape), lambda c: (c,) + (0,) * len(shape))
    return pl.pallas_call(
        denominator_kernel,
        out_shape=jax.ShapeDtypeStruct((channels, 1, mine), F32),
        grid=(channels // block,),
        in_specs=[whole(2, mine, inputs), whole(2, inputs), whole(1, inputs)],
        out_specs=whole(1, mine),
        cost_estimate=pl.CostEstimate(
            flops=16 * model.size, bytes_accessed=2 * model.size, transcendentals=0
        ),
        name="denominators",
    )(model, gains, flags)


def correlate_kernel(beam_ref, x_ref, own_ref, model_ref, gain_ref, older_ref, flag_ref, denom_ref, vis_ref, new_ref):
    for c in range(x_ref.shape[0]):
        x, own = x_ref[c], own_ref[c]
        half = x.shape[0] // 2
        exact = half & (half - 1) == 0
        before, after = (1.0 / half, 1.0) if exact else (1.0, 1.0 / half)
        scaled = (own.astype(F32) * before).astype(BF16)
        rotated = jnp.concatenate([scaled[half:], -scaled[:half]], axis=0)
        for part, left in enumerate((scaled, rotated)):
            terms = lax.dot_general(left, x, TN, preferred_element_type=F32)
            vis_ref[c, part] = (terms if exact else terms * after).astype(BF16)
        numer = numerators(x, own, model_ref.at[c], gain_ref[c], flag_ref[c].astype(F32))
        new_ref[c] = damped(older_ref[c], numer, denom_ref[c])


def update_kernel(beam_ref, x_ref, own_ref, model_ref, gain_ref, older_ref, flag_ref, new_ref):
    for c in range(x_ref.shape[0]):
        model, gains, flags = model_ref.at[c], gain_ref[c], flag_ref[c].astype(F32)
        numer = numerators(x_ref[c], own_ref[c], model, gains, flags)
        new_ref[c] = damped(older_ref[c], numer, denominators(model, gains, flags))


def turn_kernel(me_ref, in_ref, out_ref, rows_ref, *, inputs, chans, times):
    beams, _, paired, lanes = in_ref.shape
    frames = lanes // inputs
    planes = times * frames
    width = rows_ref.shape[2]
    for b in range(beams):
        for z in range(chans):
            column = (z * beams + b) * inputs
            at = column % width
            for t in range(times):
                slab = in_ref[b, (z * times + t) ^ me_ref[0]].astype(F32)
                for f in range(frames):
                    plane = t * frames + f
                    rows_ref[
                        column // width, plane * paired : (plane + 1) * paired, at : at + inputs
                    ] = slab[:, f * inputs : (f + 1) * inputs]

    def gather(k, carry):
        for q in range(rows_ref.shape[0]):
            parts = [
                rows_ref.at[q][pl.ds(s * (paired // 2) + k, planes, stride=paired), :]
                for s in range(2)
            ]
            out_ref[k, :, q * width : (q + 1) * width] = jnp.concatenate(parts, axis=0).astype(BF16)
        return carry

    lax.fori_loop(0, paired // 2, gather, 0)


def turn(me, joined, inputs, chans, times):
    beams, _, paired, lanes = joined.shape
    planes = times * (lanes // inputs)
    total = chans * beams * inputs
    width = 128
    whole = lambda *shape: pl.BlockSpec(shape, lambda c, m: (0,) * len(shape))
    out_dims = (paired // 2, 2 * planes, total)
    return pl.pallas_call(
        functools.partial(turn_kernel, inputs=inputs, chans=chans, times=times),
        out_shape=jax.ShapeDtypeStruct(out_dims, BF16),
        grid_spec=pltpu.PrefetchScalarGridSpec(
            num_scalar_prefetch=1,
            grid=(1,),
            in_specs=[whole(*joined.shape)],
            out_specs=whole(*out_dims),
            scratch_shapes=[pltpu.VMEM((total // width, planes * paired, width), F32)],
        ),
        cost_estimate=pl.CostEstimate(
            flops=0, bytes_accessed=8 * joined.size, transcendentals=0
        ),
        name="turn",
    )(me, joined)


def exchange(blocks, me, axes):
    owners = blocks.shape[0]
    if owners > 8 or owners & (owners - 1):
        mixed = lax.all_to_all(blocks, axes, split_axis=0, concat_axis=0, tiled=True)
        return [mixed], jnp.zeros_like(me)
    parts = []
    for step in range(owners):
        block = lax.dynamic_slice_in_dim(blocks, me ^ step, 1, 0)
        if step:
            block = lax.ppermute(block, axes, [(i, i ^ step) for i in range(owners)])
        parts.append(block)
    return parts, me


def gain_call(beam_index, x, model, gains, older, flags, denom=None):
    correlate = denom is not None
    channels, rows, inputs = x.shape
    mine = model.shape[2]
    block = math.gcd(channels, 4)
    whole = lambda *shape: pl.BlockSpec((block, *shape), lambda c, b: (c,) + (0,) * len(shape))
    part = lambda r: pl.BlockSpec((block, r, mine), lambda c, b: (c, 0, b[0]))
    older_spec = part(2) if older.shape[2] == inputs else whole(2, mine)
    new_shape = jax.ShapeDtypeStruct((channels, 2, mine), F32)
    if correlate:
        out_shape = [jax.ShapeDtypeStruct(model.shape, BF16), new_shape]
        out_specs = [whole(2, mine, inputs), whole(2, mine)]
    else:
        out_shape, out_specs = new_shape, whole(2, mine)
    return pl.pallas_call(
        correlate_kernel if correlate else update_kernel,
        out_shape=out_shape,
        grid_spec=pltpu.PrefetchScalarGridSpec(
            num_scalar_prefetch=1,
            grid=(channels // block,),
            in_specs=[whole(rows, inputs), part(rows), whole(2, mine, inputs), whole(2, inputs),
                      older_spec, whole(1, inputs)] + [whole(1, mine)] * correlate,
            out_specs=out_specs,
        ),
        cost_estimate=pl.CostEstimate(
            flops=8 * channels * mine * inputs * rows,
            bytes_accessed=(4 + 4 * correlate) * model.size // 2,
            transcendentals=0,
        ),
        name="correlate" if correlate else "update",
    )(beam_index, x, x, model, gains, older, flags, *([denom] if correlate else []))


def steering_kernel(base_ref, bits_ref, rot_r, rot_i, cur_r, cur_i, one_r, one_i, *, unit):
    block = rot_r.shape[0]
    beams, inputs = cur_r.shape
    step = 16

    @pl.when(pl.program_id(0) == 0)
    def _():
        first = base_ref[0]

        def fill(r, carry):
            rows = pl.ds(r * 8, 8)
            bits = bits_ref[rows, :]
            angle = (bits * first).astype(F32) * unit
            cur_r[rows, :] = jnp.cos(angle)
            cur_i[rows, :] = jnp.sin(angle)
            small = bits.astype(F32) * unit
            one_r[rows, :] = jnp.cos(small)
            one_i[rows, :] = jnp.sin(small)
            return carry

        lax.fori_loop(0, beams // 8, fill, 0)

    def advance(r, carry):
        rows = pl.ds(r * step, step)
        ar, ai = cur_r[rows, :], cur_i[rows, :]
        br, bi = one_r[rows, :], one_i[rows, :]
        for c in range(block):
            rot_r[c, rows, :] = ar.astype(BF16)
            rot_i[c, rows, :] = ai.astype(BF16)
            ar, ai = ar * br - ai * bi, ar * bi + ai * br
        cur_r[rows, :] = ar
        cur_i[rows, :] = ai
        return carry

    lax.fori_loop(0, beams // step, advance, 0)


def steering(beam_steering, inputs, channels, first_channel, chan_total):
    beams = beam_steering.shape[1]
    positions = jnp.arange(inputs, dtype=jnp.int32)
    column = positions // (inputs // 4)
    within = positions % (inputs // 4)
    bits = (
        beam_steering[0][:, None] * column[None, :] * 64
        + beam_steering[1][:, None] * within[None, :]
    ) % 256
    block = math.gcd(channels, 8)
    rot = jax.ShapeDtypeStruct((channels, beams, inputs), BF16)
    rot_spec = pl.BlockSpec((block, beams, inputs), lambda c, b: (c, 0, 0))
    return pl.pallas_call(
        functools.partial(steering_kernel, unit=2.0 * math.pi / (512 * chan_total)),
        out_shape=[rot, rot],
        grid_spec=pltpu.PrefetchScalarGridSpec(
            num_scalar_prefetch=1,
            grid=(channels // block,),
            in_specs=[pl.BlockSpec((beams, inputs), lambda c, b: (0, 0))],
            out_specs=[rot_spec, rot_spec],
            scratch_shapes=[pltpu.VMEM((beams, inputs), F32)] * 4,
        ),
        cost_estimate=pl.CostEstimate(
            flops=8 * rot.size, bytes_accessed=6 * rot.size, transcendentals=0
        ),
        name="steering",
    )(jnp.reshape(chan_total + first_channel, (1,)), bits)


def beam_kernel(x_ref, gain_ref, flag_ref, rot_r, rot_i, power_ref, *, scale):
    for c in range(x_ref.shape[0]):
        x, gains = x_ref[c], gain_ref[c]
        flags = flag_ref[c].astype(F32) * scale
        half = x.shape[0] // 2
        hr, hi = gains[0:1] * flags, gains[1:2] * flags
        xr, xi = x[:half].astype(F32), x[half:].astype(F32)
        v = complex_product(rot_r[c], rot_i[c], xr * hr - xi * hi, xi * hr + xr * hi)
        vr, vi = v[:half], v[half:]
        power_ref[c] = vr * vr + vi * vi


def form_beams(x, gains, flags, rot_r, rot_i):
    channels, rows, inputs = x.shape
    beams = rot_r.shape[1]
    block = math.gcd(channels, 4)
    whole = lambda *shape: pl.BlockSpec((block, *shape), lambda c: (c,) + (0,) * len(shape))
    return pl.pallas_call(
        functools.partial(beam_kernel, scale=1.0 / math.sqrt(inputs)),
        out_shape=jax.ShapeDtypeStruct((channels, rows // 2, beams), F32),
        grid=(channels // block,),
        in_specs=[whole(rows, inputs), whole(2, inputs), whole(1, inputs),
                  whole(beams, inputs), whole(beams, inputs)],
        out_specs=whole(rows // 2, beams),
        cost_estimate=pl.CostEstimate(
            flops=8 * channels * beams * inputs * rows,
            bytes_accessed=4 * rot_r.size, transcendentals=0,
        ),
        name="beams",
    )(x, gains, flags, rot_r, rot_i)


def shards(samples, window_taps, sky_model, prior_gains, beam_steering, input_flags):
    local_inputs = samples.shape[0]
    frames = samples.shape[3]
    kept_count = NCH
    time_count = lax.axis_size("tm")
    chan_count = lax.axis_size("chan")
    beam_count = lax.axis_size("beam")
    owners = time_count * chan_count
    chan_local = kept_count // owners
    me = (lax.axis_index("chan") * time_count + lax.axis_index("tm")).astype(jnp.int32)
    flags = input_flags[:, None, :]
    denom = first_denominators(sky_model, prior_gains, flags)
    real, imag, denom = filter_bank(samples, window_taps, kept_count, denom)
    by_owner = (owners, chan_local, frames * local_inputs)
    spectra = jnp.concatenate([real.reshape(by_owner), imag.reshape(by_owner)], axis=1)
    spectra, beam_steering = lax.optimization_barrier((spectra, beam_steering))
    parts, origin = exchange(spectra, me, ("chan", "tm"))
    input_count = local_inputs * chan_count * beam_count
    rot_r, rot_i = steering(
        beam_steering, input_count, chan_local, me * chan_local, kept_count
    )
    parts, rot_r, rot_i = lax.optimization_barrier((parts, rot_r, rot_i))
    joined = lax.all_gather(jnp.concatenate(parts, axis=0), "beam", axis=0)
    x = turn(jnp.reshape(origin, (1,)), joined, local_inputs, chan_count, time_count)
    beam_index = jnp.reshape(lax.axis_index("beam"), (1,)).astype(jnp.int32)
    visibilities, updated = gain_call(
        beam_index, x, sky_model, prior_gains, prior_gains, flags, denom
    )
    beam_power = form_beams(x, prior_gains, flags, rot_r, rot_i)
    for _ in range(ITERS - 1):
        current = lax.all_gather(updated, "beam", axis=2, tiled=True)
        updated = gain_call(beam_index, x, sky_model, current, updated, flags)
    return (visibilities, updated, jnp.transpose(beam_power, (0, 2, 1)))


def solution(mesh):
    return jax.shard_map(
        shards,
        mesh=mesh,
        in_specs=(
            P(("group", "chan", "beam"), None, None, "tm"),
            P(),
            P(("group", "chan", "tm"), None, "beam", None),
            P(("group", "chan", "tm"), None, None),
            P(None, ("group", "beam")),
            P(("group", "chan", "tm"), None),
        ),
        out_specs=(
            P(("group", "chan", "tm"), None, "beam", None),
            P(("group", "chan", "tm"), None, "beam"),
            P(("group", "chan", "tm"), "beam", None),
        ),
        check_vma=False,
    )
```

```python
import functools
import math

import jax
import jax.numpy as jnp
from jax import lax
from jax.experimental import pallas as pl
from jax.experimental.pallas import tpu as pltpu
from jax.sharding import PartitionSpec as P

NCH = 512
ITERS = 2


damping = 0.5
epsilon = 1e-06
F32 = jnp.float32
BF16 = jnp.bfloat16


def from_behind(block, axis, distance):
    devices = range(lax.axis_size(axis))
    route = [(i - distance, i) for i in devices if i - distance in devices]
    return lax.ppermute(block, axis, route)


def unit_rows(rows, columns, transform_count):
    phases = (rows[:, None] * columns[None, :] % transform_count).astype(F32) * (
        2.0 * math.pi / transform_count
    )
    return jnp.cos(phases), jnp.sin(phases)


def transform_table(kept_count, transform_count):
    fine = 1 << ((kept_count.bit_length() - 1) // 2)
    coarse = kept_count // fine
    columns = jnp.arange(transform_count, dtype=jnp.int32)
    high_c, high_s = unit_rows(jnp.arange(coarse, dtype=jnp.int32) * fine, columns, transform_count)
    low_c, low_s = unit_rows(jnp.arange(fine, dtype=jnp.int32), columns, transform_count)
    high_c, high_s, low_c, low_s = lax.optimization_barrier((high_c, high_s, low_c, low_s))
    scale = 1.0 / math.sqrt(transform_count)
    high_c, high_s = high_c * scale, high_s * scale
    cosine = high_c[:, None] * low_c[None] - high_s[:, None] * low_s[None]
    sine = high_s[:, None] * low_c[None] + high_c[:, None] * low_s[None]
    cosine = cosine.reshape(kept_count, transform_count).astype(BF16)
    sine = sine.reshape(kept_count, transform_count).astype(BF16)
    return cosine, sine


def filter_bank(samples, window_taps, kept_count, beside):
    local_inputs, _, transform_count, frames = samples.shape
    tap_count = window_taps.shape[0]
    framed = jnp.transpose(samples, (3, 1, 0, 2))
    previous = from_behind(framed[frames - tap_count + 1 :], "tm", 1)
    previous, beside = lax.optimization_barrier((previous, beside))
    extended = jnp.concatenate([previous, framed], axis=0).astype(F32)
    windowed = sum(
        extended[tap : tap + frames] * window_taps[tap][None, None, None, :]
        for tap in range(tap_count)
    )
    windowed = windowed.astype(BF16)
    real_in = windowed[:, 0].reshape(frames * local_inputs, transform_count)
    imag_in = windowed[:, 1].reshape(frames * local_inputs, transform_count)
    cosine, sine = transform_table(kept_count, transform_count)
    real = dot_nt(cosine, real_in) + dot_nt(sine, imag_in)
    imag = dot_nt(cosine, imag_in) - dot_nt(sine, real_in)
    return real.astype(BF16), imag.astype(BF16), beside


NT = (((1,), (1,)), ((), ()))
TN = (((0,), (0,)), ((), ()))


def dot_nt(a, b):
    return lax.dot_general(a, b, NT, preferred_element_type=F32)


def complex_product(left_r, left_i, vr, vi):
    straight = jnp.concatenate([vr, vi], axis=0).astype(BF16)
    crossed = jnp.concatenate([-vi, vr], axis=0).astype(BF16)
    return (dot_nt(left_r, straight) + dot_nt(left_i, crossed)).T


def numerators(x, own, model, gains, flags):
    half = x.shape[0] // 2
    hr, hi = gains[0:1] * flags, gains[1:2] * flags
    xr, xi = x[:half].astype(F32), x[half:].astype(F32)
    z = complex_product(model[0], model[1], xr * hr + xi * hi, xi * hr - xr * hi)
    zr, zi = z[:half], z[half:]
    pr, pi = own[:half].astype(F32), own[half:].astype(F32)
    numer_r = jnp.sum(pr * zr + pi * zi, axis=0, keepdims=True) * (1.0 / half)
    numer_i = jnp.sum(pi * zr - pr * zi, axis=0, keepdims=True) * (1.0 / half)
    return jnp.concatenate([numer_r, numer_i], axis=0)


def denominators(model, gains, flags):
    power = flags * (gains[0:1] * gains[0:1] + gains[1:2] * gains[1:2])
    top = power.astype(BF16).astype(F32)
    wide = (8, top.shape[1])
    both = jnp.concatenate(
        [jnp.broadcast_to(top, wide), jnp.broadcast_to(power - top, wide)], axis=0
    ).astype(BF16)
    mr, mi = model[0], model[1]
    d = dot_nt(mr * mr + mi * mi, both).T
    return d[0:1] + d[8:9] + epsilon


def damped(older, numer, denom):
    return damping * older + (1.0 - damping) * (numer / denom)


def denominator_kernel(model_ref, gain_ref, flag_ref, out_ref):
    for c in range(model_ref.shape[0]):
        out_ref[c] = denominators(model_ref.at[c], gain_ref[c], flag_ref[c].astype(F32))


def first_denominators(model, gains, flags):
    channels, _, mine, inputs = model.shape
    block = math.gcd(channels, 8)
    whole = lambda *shape: pl.BlockSpec((block, *shape), lambda c: (c,) + (0,) * len(shape))
    return pl.pallas_call(
        denominator_kernel,
        out_shape=jax.ShapeDtypeStruct((channels, 1, mine), F32),
        grid=(channels // block,),
        in_specs=[whole(2, mine, inputs), whole(2, inputs), whole(1, inputs)],
        out_specs=whole(1, mine),
        cost_estimate=pl.CostEstimate(
            flops=16 * model.size, bytes_accessed=2 * model.size, transcendentals=0
        ),
        name="denominators",
    )(model, gains, flags)


def correlate_kernel(beam_ref, x_ref, own_ref, model_ref, gain_ref, older_ref, flag_ref, denom_ref, vis_ref, new_ref):
    for c in range(x_ref.shape[0]):
        x, own = x_ref[c], own_ref[c]
        half = x.shape[0] // 2
        exact = half & (half - 1) == 0
        before, after = (1.0 / half, 1.0) if exact else (1.0, 1.0 / half)
        scaled = (own.astype(F32) * before).astype(BF16)
        rotated = jnp.concatenate([scaled[half:], -scaled[:half]], axis=0)
        for part, left in enumerate((scaled, rotated)):
            terms = lax.dot_general(left, x, TN, preferred_element_type=F32)
            vis_ref[c, part] = (terms if exact else terms * after).astype(BF16)
        numer = numerators(x, own, model_ref.at[c], gain_ref[c], flag_ref[c].astype(F32))
        new_ref[c] = damped(older_ref[c], numer, denom_ref[c])


def update_kernel(beam_ref, x_ref, own_ref, model_ref, gain_ref, older_ref, flag_ref, new_ref):
    for c in range(x_ref.shape[0]):
        model, gains, flags = model_ref.at[c], gain_ref[c], flag_ref[c].astype(F32)
        numer = numerators(x_ref[c], own_ref[c], model, gains, flags)
        new_ref[c] = damped(older_ref[c], numer, denominators(model, gains, flags))


def turn_kernel(me_ref, in_ref, out_ref, rows_ref, *, inputs, chans, times):
    beams, _, paired, lanes = in_ref.shape
    frames = lanes // inputs
    planes = times * frames
    width = rows_ref.shape[2]
    for b in range(beams):
        for z in range(chans):
            column = (z * beams + b) * inputs
            at = column % width
            for t in range(times):
                slab = in_ref[b ^ me_ref[1], (z * times + t) ^ me_ref[0]].astype(F32)
                for f in range(frames):
                    plane = t * frames + f
                    rows_ref[
                        column // width, plane * paired : (plane + 1) * paired, at : at + inputs
                    ] = slab[:, f * inputs : (f + 1) * inputs]

    def gather(k, carry):
        for q in range(rows_ref.shape[0]):
            parts = [
                rows_ref.at[q][pl.ds(s * (paired // 2) + k, planes, stride=paired), :]
                for s in range(2)
            ]
            out_ref[k, :, q * width : (q + 1) * width] = jnp.concatenate(parts, axis=0).astype(BF16)
        return carry

    lax.fori_loop(0, paired // 2, gather, 0)


def turn(me, joined, inputs, chans, times):
    beams, _, paired, lanes = joined.shape
    planes = times * (lanes // inputs)
    total = chans * beams * inputs
    width = 128
    whole = lambda *shape: pl.BlockSpec(shape, lambda c, m: (0,) * len(shape))
    out_dims = (paired // 2, 2 * planes, total)
    return pl.pallas_call(
        functools.partial(turn_kernel, inputs=inputs, chans=chans, times=times),
        out_shape=jax.ShapeDtypeStruct(out_dims, BF16),
        grid_spec=pltpu.PrefetchScalarGridSpec(
            num_scalar_prefetch=1,
            grid=(1,),
            in_specs=[whole(*joined.shape)],
            out_specs=whole(*out_dims),
            scratch_shapes=[pltpu.VMEM((total // width, planes * paired, width), F32)],
        ),
        cost_estimate=pl.CostEstimate(
            flops=0, bytes_accessed=8 * joined.size, transcendentals=0
        ),
        name="turn",
    )(me, joined)


def other_core(block):
    return lax.ppermute(block, "beam", [(0, 1), (1, 0)])


def exchange(blocks, me, axes):
    owners = blocks.shape[0]
    if owners > 8 or owners & (owners - 1):
        mixed = lax.all_to_all(blocks, axes, split_axis=0, concat_axis=0, tiled=True)
        return [mixed], jnp.zeros_like(me)
    parts = []
    for step in range(owners):
        block = lax.dynamic_slice_in_dim(blocks, me ^ step, 1, 0)
        if step:
            block = lax.ppermute(block, axes, [(i, i ^ step) for i in range(owners)])
        parts.append(block)
    return parts, me


def gain_call(beam_index, x, model, gains, older, flags, denom=None):
    correlate = denom is not None
    channels, rows, inputs = x.shape
    mine = model.shape[2]
    block = math.gcd(channels, 8)
    whole = lambda *shape: pl.BlockSpec((block, *shape), lambda c, b: (c,) + (0,) * len(shape))
    part = lambda r: pl.BlockSpec((block, r, mine), lambda c, b: (c, 0, b[0]))
    older_spec = part(2) if older.shape[2] == inputs else whole(2, mine)
    new_shape = jax.ShapeDtypeStruct((channels, 2, mine), F32)
    if correlate:
        out_shape = [jax.ShapeDtypeStruct(model.shape, BF16), new_shape]
        out_specs = [whole(2, mine, inputs), whole(2, mine)]
    else:
        out_shape, out_specs = new_shape, whole(2, mine)
    return pl.pallas_call(
        correlate_kernel if correlate else update_kernel,
        out_shape=out_shape,
        grid_spec=pltpu.PrefetchScalarGridSpec(
            num_scalar_prefetch=1,
            grid=(channels // block,),
            in_specs=[whole(rows, inputs), part(rows), whole(2, mine, inputs), whole(2, inputs),
                      older_spec, whole(1, inputs)] + [whole(1, mine)] * correlate,
            out_specs=out_specs,
        ),
        cost_estimate=pl.CostEstimate(
            flops=8 * channels * mine * inputs * rows,
            bytes_accessed=(4 + 4 * correlate) * model.size // 2,
            transcendentals=0,
        ),
        name="correlate" if correlate else "update",
    )(beam_index, x, x, model, gains, older, flags, *([denom] if correlate else []))


def steering_kernel(base_ref, bits_ref, rot_r, rot_i, cur_r, cur_i, one_r, one_i, *, unit):
    block = rot_r.shape[0]
    beams, inputs = cur_r.shape
    step = 16

    @pl.when(pl.program_id(0) == 0)
    def _():
        first = base_ref[0]

        def fill(r, carry):
            rows = pl.ds(r * 8, 8)
            bits = bits_ref[rows, :]
            angle = (bits * first).astype(F32) * unit
            cur_r[rows, :] = jnp.cos(angle)
            cur_i[rows, :] = jnp.sin(angle)
            small = bits.astype(F32) * unit
            one_r[rows, :] = jnp.cos(small)
            one_i[rows, :] = jnp.sin(small)
            return carry

        lax.fori_loop(0, beams // 8, fill, 0)

    def advance(r, carry):
        rows = pl.ds(r * step, step)
        ar, ai = cur_r[rows, :], cur_i[rows, :]
        br, bi = one_r[rows, :], one_i[rows, :]
        for c in range(block):
            rot_r[c, rows, :] = ar.astype(BF16)
            rot_i[c, rows, :] = ai.astype(BF16)
            ar, ai = ar * br - ai * bi, ar * bi + ai * br
        cur_r[rows, :] = ar
        cur_i[rows, :] = ai
        return carry

    lax.fori_loop(0, beams // step, advance, 0)


def steering(beam_steering, inputs, channels, first_channel, chan_total):
    beams = beam_steering.shape[1]
    positions = jnp.arange(inputs, dtype=jnp.int32)
    column = positions // (inputs // 4)
    within = positions % (inputs // 4)
    bits = (
        beam_steering[0][:, None] * column[None, :] * 64
        + beam_steering[1][:, None] * within[None, :]
    ) % 256
    block = math.gcd(channels, 8)
    rot = jax.ShapeDtypeStruct((channels, beams, inputs), BF16)
    rot_spec = pl.BlockSpec((block, beams, inputs), lambda c, b: (c, 0, 0))
    return pl.pallas_call(
        functools.partial(steering_kernel, unit=2.0 * math.pi / (512 * chan_total)),
        out_shape=[rot, rot],
        grid_spec=pltpu.PrefetchScalarGridSpec(
            num_scalar_prefetch=1,
            grid=(channels // block,),
            in_specs=[pl.BlockSpec((beams, inputs), lambda c, b: (0, 0))],
            out_specs=[rot_spec, rot_spec],
            scratch_shapes=[pltpu.VMEM((beams, inputs), F32)] * 4,
        ),
        cost_estimate=pl.CostEstimate(
            flops=8 * rot.size, bytes_accessed=6 * rot.size, transcendentals=0
        ),
        name="steering",
    )(jnp.reshape(chan_total + first_channel, (1,)), bits)


def beam_kernel(x_ref, gain_ref, flag_ref, rot_r, rot_i, power_ref, *, scale):
    for c in range(x_ref.shape[0]):
        x, gains = x_ref[c], gain_ref[c]
        flags = flag_ref[c].astype(F32) * scale
        half = x.shape[0] // 2
        hr, hi = gains[0:1] * flags, gains[1:2] * flags
        xr, xi = x[:half].astype(F32), x[half:].astype(F32)
        v = complex_product(rot_r[c], rot_i[c], xr * hr - xi * hi, xi * hr + xr * hi)
        vr, vi = v[:half], v[half:]
        power_ref[c] = vr * vr + vi * vi


def form_beams(x, gains, flags, rot_r, rot_i):
    channels, rows, inputs = x.shape
    beams = rot_r.shape[1]
    block = math.gcd(channels, 16)
    whole = lambda *shape: pl.BlockSpec((block, *shape), lambda c: (c,) + (0,) * len(shape))
    return pl.pallas_call(
        functools.partial(beam_kernel, scale=1.0 / math.sqrt(inputs)),
        out_shape=jax.ShapeDtypeStruct((channels, rows // 2, beams), F32),
        grid=(channels // block,),
        in_specs=[whole(rows, inputs), whole(2, inputs), whole(1, inputs),
                  whole(beams, inputs), whole(beams, inputs)],
        out_specs=whole(rows // 2, beams),
        cost_estimate=pl.CostEstimate(
            flops=8 * channels * beams * inputs * rows,
            bytes_accessed=4 * rot_r.size, transcendentals=0,
        ),
        name="beams",
    )(x, gains, flags, rot_r, rot_i)


def shards(samples, window_taps, sky_model, prior_gains, beam_steering, input_flags):
    local_inputs = samples.shape[0]
    frames = samples.shape[3]
    kept_count = NCH
    time_count = lax.axis_size("tm")
    chan_count = lax.axis_size("chan")
    beam_count = lax.axis_size("beam")
    owners = time_count * chan_count
    chan_local = kept_count // owners
    me = (lax.axis_index("chan") * time_count + lax.axis_index("tm")).astype(jnp.int32)
    flags = input_flags[:, None, :]
    denom = first_denominators(sky_model, prior_gains, flags)
    real, imag, denom = filter_bank(samples, window_taps, kept_count, denom)
    by_owner = (owners, chan_local, frames * local_inputs)
    spectra = jnp.concatenate([real.reshape(by_owner), imag.reshape(by_owner)], axis=1)
    spectra, beam_steering = lax.optimization_barrier((spectra, beam_steering))
    parts, origin = exchange(spectra, me, ("chan", "tm"))
    input_count = local_inputs * chan_count * beam_count
    rot_r, rot_i = steering(
        beam_steering, input_count, chan_local, me * chan_local, kept_count
    )
    parts, rot_r, rot_i = lax.optimization_barrier((parts, rot_r, rot_i))
    beam = lax.axis_index("beam").astype(jnp.int32)
    mixed = jnp.concatenate(parts, axis=0)
    if beam_count == 2:
        joined, core = jnp.stack([mixed, other_core(mixed)]), beam
    else:
        joined, core = lax.all_gather(mixed, "beam", axis=0), jnp.zeros_like(beam)
    x = turn(jnp.stack([origin, core]), joined, local_inputs, chan_count, time_count)
    beam_index = jnp.reshape(lax.axis_index("beam"), (1,)).astype(jnp.int32)
    visibilities, updated = gain_call(
        beam_index, x, sky_model, prior_gains, prior_gains, flags, denom
    )
    beam_power = form_beams(x, prior_gains, flags, rot_r, rot_i)
    for _ in range(ITERS - 1):
        if beam_count == 2:
            other, beam_power = lax.optimization_barrier((other_core(updated), beam_power))
            current = jnp.where(
                beam == 0,
                jnp.concatenate([updated, other], axis=2),
                jnp.concatenate([other, updated], axis=2),
            )
        else:
            current = lax.all_gather(updated, "beam", axis=2, tiled=True)
        updated = gain_call(beam_index, x, sky_model, current, updated, flags)
    return (visibilities, updated, jnp.transpose(beam_power, (0, 2, 1)))


def solution(mesh):
    return jax.shard_map(
        shards,
        mesh=mesh,
        in_specs=(
            P(("group", "chan", "beam"), None, None, "tm"),
            P(),
            P(("group", "chan", "tm"), None, "beam", None),
            P(("group", "chan", "tm"), None, None),
            P(None, ("group", "beam")),
            P(("group", "chan", "tm"), None),
        ),
        out_specs=(
            P(("group", "chan", "tm"), None, "beam", None),
            P(("group", "chan", "tm"), None, "beam"),
            P(("group", "chan", "tm"), "beam", None),
        ),
        check_vma=False,
    )
```
